32 devices in a mesh: ctx: 16 (over z, y, core), mp: 2 (over x).
Axes of the slice: x: 2, y: 2, z: 4, core: 2. Of those that a mesh axis runs over, the one named last changes fastest.
Arguments:
- features: bfloat16 [3, 8192, 4096], P(None, 'ctx', 'mp'), may hold values from -6 to 6
- short_filter: float32 [3, 7, 4096], P(None, None, 'mp'), may hold values from -2 to 2
- residues: float32 [4096, 16], P('mp'), may hold values from -1.5 to 1.5
- rates: float32 [4096, 16], P('mp'), as said below
- out_weight: bfloat16 [4096, 4096], P('ctx', 'mp'), may hold values from -0.125 to 0.125
Outputs:
- mixed: bfloat16 [8192, 4096], P('ctx', 'mp')
The draws below stay inside these ranges and needn't reach their ends.
Inputs may be any that keep to these rules, and one draw needn't show every extreme that they name: `rates`: every rate lies between 0.3 / 8192 and 0.08.
All inputs are finite; a program needn't handle non-finite values.
Results may differ from the reference program's by a relative error of at most 0.0058.
Values may be sent and summed in bfloat16 or wider, within the bound.
A program may use at most 128 MiB of HBM per device.

```python
import math
import jax
import jax.numpy as jnp
from jax import lax

D = 4096
MODES = 16
KERNEL = 7
BLOCK = 128
TOKENS = 8192


def draw_rates(key, part):
    pick_key, slow_key, fast_key = jax.random.split(key, 3)
    slow_rates = jnp.exp(jax.random.uniform(slow_key, (D, MODES), jnp.float32, math.log(0.3 / TOKENS), math.log(2.0 / TOKENS)))
    fast_rates = jnp.exp(jax.random.uniform(fast_key, (D, MODES), jnp.float32, math.log(0.05), math.log(0.08)))
    share = 0.5
    chosen = jax.random.uniform(pick_key, (D, MODES), jnp.float32) < share
    return jnp.where(chosen, slow_rates, fast_rates).astype(jnp.float32)


def with_spikes(values, key, source, target, shards_of, factor):
    owner, partner = [(jnp.arange(values.shape[axis_at]) // (values.shape[axis_at] // shards_of)).reshape([-1 if axis == axis_at else 1 for axis in range(values.ndim)]) for axis_at in (source, target)]
    chosen = jax.random.permutation(key, shards_of)[partner]
    strong = (owner == chosen) | (owner == (partner + shards_of // 2) % shards_of)
    return jnp.where(strong, factor * values, values)


def shard_levels(rng, extent, pieces, least, high):
    def one(dim, parts):
        draws = jax.random.uniform(jax.random.fold_in(jax.random.fold_in(rng, 6), dim), (parts,), jnp.float32, least / len(pieces), high / len(pieces))
        return jnp.repeat(jnp.exp(draws), extent[dim] // parts).reshape((-1,) + (1,) * (len(extent) - dim - 1))

    gain = one(*pieces[0])
    for cut in pieces[1:]:
        gain = gain * one(*cut)
    return gain


def scatter_about(stream_key, extent, scale, bound, cuts=(), kind=jnp.bfloat16):
    factor_of = shard_levels(stream_key, extent, cuts, -0.22, 0.18) if cuts else 1.0
    drawn = jax.random.normal(stream_key, extent, jnp.float32) * scale * factor_of
    return jnp.minimum(jnp.maximum(drawn, -bound), bound).astype(kind)


def bell_draw_with(key, shape, scale, limit, shards, heavy, kind=jnp.bfloat16):
    values = scale * jax.random.normal(key, shape, jnp.float32)
    if shards:
        values = values * shard_levels(key, shape, shards, -0.22, 0.18)
    return jnp.clip(with_spikes(values, jax.random.fold_in(key, 3), *heavy), -limit, limit).astype(kind)


def setup_inputs(seed: int = 0) -> dict:
    key_of = jax.random.split(jax.random.key(seed), 6)
    features = scatter_about(key_of[0], (3, TOKENS, D), 1.0, 6.0, ((1, 16), (2, 2)))
    short_filter = scatter_about(key_of[1], (3, KERNEL, D), KERNEL ** -0.5, 2.0, ((2, 2),), jnp.float32)
    residues = scatter_about(key_of[2], (D, MODES), 0.25, 1.5, ((0, 2),), jnp.float32)
    rates = draw_rates(jax.random.fold_in(key_of[5], 71), 0)
    out_weight = bell_draw_with(key_of[4], (D, D), D ** -0.5, 0.125, ((0, 16), (1, 2)), (0, 1, 16, 2.0))
    return dict(features=features, short_filter=short_filter, residues=residues, rates=rates, out_weight=out_weight)


def short_conv(extended, taps, length):
    width = taps.shape[1]
    running = jnp.zeros((extended.shape[0], length, extended.shape[2]), jnp.float32)
    for offset in range(width):
        window = extended[:, width - 1 - offset:width - 1 - offset + length, :].astype(jnp.float32)
        running = running + taps[:, offset, None, :] * window
    return running

def reference(features, short_filter, residues, rates, out_weight):
    width = short_filter.shape[1]
    block_width = 128 if D % 128 == 0 else D
    groups = D // block_width
    count = TOKENS // BLOCK
    positions = jnp.arange(BLOCK, dtype=jnp.float32)
    lag_table = jnp.arange(BLOCK, dtype=jnp.int32)[:, None] - jnp.arange(BLOCK, dtype=jnp.int32)[None, :]
    causal = lag_table >= 0
    clipped = jnp.maximum(lag_table, 0)

    def one_group(packed):
        stream, taps, group_residues, group_rates = packed
        padded = jnp.pad(stream, ((0, 0), (width - 1, 0), (0, 0)))
        featured = short_conv(padded, taps, TOKENS)
        gated = (featured[1] * featured[2]).astype(jnp.bfloat16)
        scaled = group_residues * jnp.sqrt(-jnp.expm1(-2.0 * group_rates))
        decays = jnp.exp(-group_rates[:, :, None] * positions[None, None, :])
        lag_filter = jnp.einsum('cn,cnl->cl', scaled, decays, precision=lax.Precision.HIGHEST)
        toeplitz = jnp.where(causal[None], lag_filter[:, clipped], jnp.float32(0.0))
        blocks = gated.reshape(count, BLOCK, block_width).astype(jnp.float32)
        local = jnp.einsum('cij,bjc->bic', toeplitz, blocks, precision=lax.Precision.HIGHEST)
        end_weights = jnp.exp(-group_rates[None] * (BLOCK - positions)[:, None, None])
        start_weights = jnp.exp(-group_rates[None] * positions[:, None, None]) * scaled[None]
        block_states = jnp.einsum('bjc,jcn->bcn', blocks, end_weights, precision=lax.Precision.HIGHEST)
        step_decay = jnp.exp(-group_rates * BLOCK)

        def advance(carried, state):
            return (step_decay * carried + state, carried)
        _, carried_all = lax.scan(advance, jnp.zeros_like(step_decay), block_states)
        far_term = jnp.einsum('icn,bcn->bic', start_weights, carried_all, precision=lax.Precision.HIGHEST)
        long_rows = (local + far_term).reshape(TOKENS, block_width)
        return (featured[0] * long_rows).astype(jnp.bfloat16)
    streams = jnp.moveaxis(features.reshape(3, TOKENS, groups, block_width), 2, 0)
    taps_all = jnp.moveaxis(short_filter.reshape(3, width, groups, block_width), 2, 0)
    outputs = lax.map(one_group, (streams, taps_all, residues.reshape(groups, block_width, MODES), rates.reshape(groups, block_width, MODES)))
    combined = jnp.moveaxis(outputs, 0, 1).reshape(TOKENS, D)
    return jnp.dot(combined, out_weight, preferred_element_type=jnp.float32).astype(jnp.bfloat16)
```

```python
import jax
import jax.numpy as jnp
from jax import lax
from jax.experimental import pallas as pl
from jax.experimental.pallas import tpu as pltpu
from jax.sharding import PartitionSpec as P

LANES = 128
ROWS = 8
STEP = 8
HALO = 16
SIDE = 2
JUMP = 2 * SIDE
F32 = jnp.float32
MESH = pl.DeviceIdType.MESH


def one_minus_exp(x):
    series = jnp.ones_like(x)
    for k in range(11, 1, -1):
        series = 1.0 - x * (1.0 / k) * series
    return jnp.where(x < 0.5, x * series, 1.0 - jnp.exp(-x))


def mixer_kernel(n, m, quarters, feat, taps, rates, residues, own_weight, out,
                 stream, halo, ext, gated, fq, inclusive, decay, scaled, level, tot, behind, carried,
                 initial, weight, combined, total,
                 w_send, w_recv, s_send, s_recv, z_send, z_recv, x_send, x_recv, h_send, h_recv,
                 f_sem, k_sem):
    length, channels = feat.shape[1:]
    width = taps.shape[1]
    modes = rates.shape[0]
    depth, wide = own_weight.shape
    seg = length // ROWS
    pitch = seg + ROWS + 1
    blocks = channels // LANES
    chips = n // 2
    line = chips // SIDE
    per_group = chips // m
    parts = per_group
    part = channels // parts
    piece = wide // quarters
    half = channels // 2
    me, mine = lax.axis_index("ctx"), lax.axis_index("mp")
    core = lax.rem(me, 2)
    chip = lax.div(me, 2)
    b = lax.rem(chip, SIDE)
    a = lax.div(chip, SIDE)
    r = b * 2 + core
    partner = me + 1 - 2 * core
    across = me + 2 * (1 - 2 * b)
    up, down = a < line - 1, a > 0

    barrier = pltpu.get_barrier_semaphore()

    def greet(other, ok):
        @pl.when(ok)
        def _():
            pl.semaphore_signal(barrier, inc=1, device_id={"ctx": other}, device_id_type=MESH)

    greet(me + 1, me + 1 < n)
    greet(me - 1, me > 0)
    pl.semaphore_signal(barrier, inc=1, device_id={"ctx": across}, device_id_type=MESH)
    for k in range(1, line):
        greet(me + k * JUMP, a + k < line)
        greet(me - k * JUMP, a >= k)
    for k in range(1, m):
        pl.semaphore_signal(
            barrier, inc=1, device_id={"mp": lax.rem(mine + k, m)}, device_id_type=MESH
        )
    pl.semaphore_wait(
        barrier,
        1 + (line - 1) + (m - 1) + (me > 0).astype(jnp.int32) + (me < n - 1).astype(jnp.int32),
    )

    def columns(q):
        return pl.ds(pl.multiple_of(q * piece, piece), piece)

    def slot(s, q):
        return weight.at[pl.ds(pl.multiple_of(s * depth, depth), depth), columns(q)]

    def push(kind, s, q, to, own=False):
        return pltpu.make_async_remote_copy(
            src_ref=own_weight.at[:, columns(q)] if own else slot(s, q),
            dst_ref=slot(s, q),
            send_sem=w_send.at[kind, s, q],
            recv_sem=w_recv.at[s, q],
            device_id={"ctx": to},
            device_id_type=MESH,
        )

    def halo_copy():
        return pltpu.make_async_remote_copy(
            src_ref=feat.at[:, length - HALO :, :],
            dst_ref=halo,
            send_sem=h_send,
            recv_sem=h_recv,
            device_id={"ctx": lax.rem(me + 1, n)},
            device_id_type=MESH,
        )

    def load(p):
        where = pl.ds(pl.multiple_of(p * part, part), part)
        return pltpu.make_async_copy(feat.at[:, :, where], stream.at[:, :, where], f_sem.at[p])

    @pl.when(me < n - 1)
    def _():
        halo_copy().start()

    load(0).start()
    for q in range(quarters):
        @pl.when(up)
        def _():
            push(0, me, q, me + JUMP, own=True).start()

        @pl.when(down)
        def _():
            push(1, me, q, me - JUMP, own=True).start()

        push(2, me, q, across, own=True).start()
    for p in range(1, parts):
        load(p).start()
    for q in range(quarters):
        push(3, me, q, partner, own=True).start()
    keep = pltpu.make_async_copy(
        own_weight, weight.at[pl.ds(pl.multiple_of(me * depth, depth), depth), :], k_sem
    )
    keep.start()

    decay[0] = jnp.exp(-rates[...])
    decay[1] = jnp.exp(-rates[...] * seg)
    scaled[...] = residues[...] * jnp.sqrt(one_minus_exp(2.0 * rates[...]))

    @pl.when(me > 0)
    def _():
        halo_copy().wait_recv()

    @pl.when(me == 0)
    def _():
        halo[...] = jnp.zeros_like(halo)

    shape = (ROWS, LANES)
    row = lax.broadcasted_iota(jnp.int32, shape, 0)

    def lanes(c):
        return pl.ds(pl.multiple_of(c * LANES, LANES), LANES)

    def featurize(c):
        cols = lanes(c)
        for i in range(3):
            ext[i, :ROWS, :] = halo[i, :, cols].astype(F32)[HALO - ROWS :, :]
            for g in range(ROWS):
                ext[i, g * pitch + ROWS : g * pitch + ROWS + seg, :] = stream[
                    i, g * seg : (g + 1) * seg, cols
                ].astype(F32)
                if g:
                    ext[i, g * pitch : g * pitch + ROWS, :] = stream[
                        i, g * seg - HALO : g * seg, cols
                    ].astype(F32)[HALO - ROWS :, :]
        tap = [
            [jnp.broadcast_to(taps[i, j : j + 1, cols], shape) for j in range(width)]
            for i in range(3)
        ]

        @pl.loop(0, seg // STEP)
        def _(block):
            start = block * STEP
            made = []
            for i in range(3):
                rows = [
                    ext[i, pl.ds(start + k + ROWS - (width - 1), ROWS, stride=pitch), :]
                    for k in range(STEP + width - 1)
                ]
                made.append(
                    [
                        sum(
                            (tap[i][j] * rows[k + width - 1 - j] for j in range(1, width)),
                            tap[i][0] * rows[k + width - 1],
                        )
                        for k in range(STEP)
                    ]
                )
            for k in range(STEP):
                at = c * seg + start + k
                fq[at] = made[0][k]
                gated[at] = (made[1][k] * made[2][k]).astype(jnp.bfloat16).astype(F32)

        step_decay = [jnp.broadcast_to(decay[0, k : k + 1, cols], shape) for k in range(modes)]

        def advance(block, modal):
            for k in range(STEP):
                g = gated[c * seg + block * STEP + k]
                modal = tuple(d * s + g for d, s in zip(step_decay, modal))
            return modal

        modal = lax.fori_loop(0, seg // STEP, advance, (jnp.zeros(shape, F32),) * modes)
        for k in range(modes):
            value = modal[k]
            factor = jnp.broadcast_to(decay[1, k : k + 1, cols], shape)
            distance = 1
            while distance < ROWS:
                earlier = pltpu.roll(value, distance, 0)
                value = value + jnp.where(row >= distance, factor * earlier, 0.0)
                factor = factor * factor
                distance *= 2
            inclusive[c * modes + k] = value
            level[r, k : k + 1, cols] = value[ROWS - 1 :, :]

    @pl.loop(0, parts)
    def _(p):
        load(p).wait()

        @pl.loop(0, blocks // parts)
        def _(j):
            featurize(p * (blocks // parts) + j)

    def take(s, q):
        push(3, s, q, partner).wait_recv()

    def via_line(at, q):
        return (at > 0) & (at < line - 1) | (q >= quarters - quarters // 2)

    def serve_line(k, q):
        for sign, kind, onward in ((1, 0, up), (-1, 1, down)):
            @pl.when((a - sign * k >= 0) & (a - sign * k < line))
            def _():
                s = me - sign * k * JUMP
                take(s, q)

                @pl.when(onward)
                def _():
                    push(kind, s, q, me + sign * JUMP).start()

                if k == 1:
                    @pl.when(jnp.logical_not(via_line(a, q)))
                    def _():
                        push(2, s, q, across).start()
                else:
                    push(2, s, q, across).start()
                push(3, s, q, partner).start()

    def cross_on(q):
        @pl.when(up & via_line(a + 1, q))
        def _():
            push(0, across, q, me + JUMP).start()

        @pl.when(down & via_line(a - 1, q))
        def _():
            push(1, across, q, me - JUMP).start()

    inside = up & down

    def serve_cross(q):
        take(across, q)
        push(3, across, q, partner).start()

        @pl.when(jnp.logical_not(inside))
        def _():
            cross_on(q)

    def state_copy(kind, src, to, dst=None):
        return pltpu.make_async_remote_copy(
            src_ref=src,
            dst_ref=src if dst is None else dst,
            send_sem=s_send.at[kind],
            recv_sem=s_recv.at[kind],
            device_id={"ctx": to},
            device_id_type=MESH,
        )

    opposite = (1 - b) * 2 + core
    to_partner = state_copy(0, level.at[r], partner)
    to_across = state_copy(1, level.at[r], across)
    to_partner_too = state_copy(2, level.at[opposite], partner)
    to_partner_last = state_copy(3, carried.at[core], partner)
    to_across.start()
    to_partner.start()

    if line > 1:
        serve_line(1, 0)
    to_across.wait_recv()
    to_partner_too.start()
    to_partner.wait_recv()
    to_partner_too.wait_recv()

    halves = pl.ds(pl.multiple_of(core * half, half), half)
    fade_device = jnp.exp(rates[:, halves] * (-1.0 * length))
    value = level[0, :, halves]
    for k in range(1, JUMP):
        value = fade_device * value + level[k, :, halves]
    tot[...] = value
    carried[core] = jnp.zeros_like(tot)

    def ahead(k):
        return pltpu.make_async_remote_copy(
            src_ref=tot,
            dst_ref=behind.at[k],
            send_sem=z_send.at[k],
            recv_sem=z_recv.at[k],
            device_id={"ctx": lax.rem(me + k * JUMP, n)},
            device_id_type=MESH,
        )

    for k in range(1, line):
        @pl.when(a + k < line)
        def _():
            ahead(k).start()

    if line > 1:
        @pl.loop(1, quarters)
        def _(q):
            serve_line(1, q)

    @pl.loop(0, quarters)
    def _(q):
        serve_cross(q)

    for k in range(1, line):
        @pl.when(a >= k)
        def _():
            ahead(k).wait_recv()
            carried[core] += behind[k] * jnp.exp(
                rates[:, halves] * (-1.0 * length * JUMP * (k - 1))
            )

    to_partner_last.start()
    to_partner_last.wait_recv()
    for h in range(2):
        where = slice(h * half, (h + 1) * half)
        fade_device = jnp.exp(rates[:, where] * (-1.0 * length))
        value = carried[h]
        for k in range(JUMP - 1):
            value = jnp.where(r > k, fade_device * value + level[k, :, where], value)
        initial[:, where] = value

    def part_of(group, i):
        first = group * (per_group // SIDE)
        step = i // SIDE
        place = jnp.where(a <= first, step, per_group // SIDE - 1 - step)
        return place * SIDE + lax.rem(b + lax.rem(i, SIDE), SIDE)

    def swap(k, p):
        where = combined.at[mine, :, pl.ds(pl.multiple_of(p * part, part), part)]
        return pltpu.make_async_remote_copy(
            src_ref=where,
            dst_ref=where,
            send_sem=x_send.at[k, p],
            recv_sem=x_recv.at[mine, p],
            device_id={"mp": lax.rem(mine + k, m)},
            device_id_type=MESH,
        )

    offset = (row * seg).astype(F32)

    def finish(c):
        cols = lanes(c)
        starts = []
        for k in range(modes):
            before = jnp.where(row == 0, 0.0, pltpu.roll(inclusive[c * modes + k], 1, 0))
            fade = jnp.exp(-rates[k : k + 1, cols] * offset)
            starts.append(before + fade * initial[k : k + 1, cols])
        step_decay = [jnp.broadcast_to(decay[0, k : k + 1, cols], shape) for k in range(modes)]
        gain = [jnp.broadcast_to(scaled[k : k + 1, cols], shape) for k in range(modes)]

        def advance(block, modal):
            for k in range(STEP):
                t = block * STEP + k
                g = gated[c * seg + t]
                modal = tuple(d * s + g for d, s in zip(step_decay, modal))
                terms = [w * s for w, s in zip(gain, modal)]
                while len(terms) > 1:
                    terms = [sum(terms[i + 1 : i + 2], terms[i]) for i in range(0, len(terms), 2)]
                ext[0, pl.ds(t, ROWS, stride=pitch), :] = fq[c * seg + t] * terms[0]
            return modal

        lax.fori_loop(0, seg // STEP, advance, tuple(starts))
        for g in range(ROWS):
            combined[mine, g * seg : (g + 1) * seg, cols] = ext[
                0, g * pitch : g * pitch + seg, :
            ].astype(jnp.bfloat16)

    beside = quarters == parts and line > 2

    @pl.loop(0, parts)
    def _(i):
        p = part_of(mine, i)

        @pl.loop(0, blocks // parts)
        def _(j):
            finish(p * (blocks // parts) + j)

        for k in range(1, m):
            swap(k, p).start()
        if beside:
            serve_line(2, i)

    if line > 2 and not beside:
        @pl.loop(0, quarters)
        def _(q):
            serve_line(2, q)

    @pl.when(inside)
    def _():
        @pl.loop(0, quarters)
        def _(q):
            cross_on(q)

    keep.wait()

    def multiply(group, i, first=False, last=False):
        p = part_of(group, i)
        which = group * per_group + p
        there = lax.div(which, SIDE)

        @pl.when((lax.rem(which, SIDE) != b) & (there != a))
        def _():
            @pl.loop(0, quarters)
            def _(q):
                take(which * 2 + core, q)
                push(3, which * 2 + core, q, partner).start()

        rows = pl.ds(pl.multiple_of(which * 2 * depth, 2 * depth), 2 * depth)
        inner = pl.ds(pl.multiple_of(p * part, part), part)

        @pl.loop(0, quarters)
        def _(q):
            take(which * 2 + 1 - core, q)
            cols = columns(q)
            product = jnp.dot(
                combined[group, :, inner], weight[rows, cols], preferred_element_type=F32
            )
            if not first:
                product = total[:, cols] + product
            if last:
                out[:, cols] = product.astype(out.dtype)
            else:
                total[:, cols] = product

    def near(i, first=False):
        multiply(mine, i, first=first)

    def other(i, last=False):
        for k in range(1, m):
            group = lax.rem(mine + k, m)
            p = part_of(group, i)
            where = combined.at[group, :, pl.ds(pl.multiple_of(p * part, part), part)]
            pltpu.make_async_remote_copy(
                src_ref=where,
                dst_ref=where,
                send_sem=x_send.at[k, p],
                recv_sem=x_recv.at[group, p],
                device_id={"mp": group},
                device_id_type=MESH,
            ).wait_recv()
            multiply(group, i, last=last and k == m - 1)

    def serve_rest(q):
        for k in range(3, line):
            serve_line(k, q)

    if parts == 4 and quarters == 4:
        near(0, first=True)
        other(0)
        serve_rest(0)
        near(1)
        serve_rest(1)
        other(1)
        serve_rest(2)
        serve_rest(3)
        near(2)
        other(2)
        near(3)
        other(3, last=True)
    else:
        @pl.loop(0, quarters)
        def _(q):
            serve_rest(q)

        for i in range(parts):
            near(i, first=i == 0)
            other(i, last=i == parts - 1)

    @pl.when(me < n - 1)
    def _():
        halo_copy().wait_send()

    for copy in (to_partner, to_across, to_partner_too, to_partner_last):
        copy.wait_send()
    for k in range(1, line):
        @pl.when(a + k < line)
        def _():
            ahead(k).wait_send()

    for k in range(1, m):
        for p in range(parts):
            swap(k, p).wait_send()

    @pl.loop(0, quarters)
    def _(q):
        @pl.when(up & via_line(a + 1, q))
        def _():
            push(0, across, q, me + JUMP).wait_send()

        @pl.when(down & via_line(a - 1, q))
        def _():
            push(1, across, q, me - JUMP).wait_send()

        @pl.loop(0, line)
        def _(aa):
            s = (aa * SIDE + b) * 2 + core
            gap = jnp.abs(aa - a)

            @pl.when(up & (aa <= a))
            def _():
                push(0, s, q, me + JUMP).wait_send()

            @pl.when(down & (aa >= a))
            def _():
                push(1, s, q, me - JUMP).wait_send()

            @pl.when((gap != 1) | jnp.logical_not(via_line(a, q)))
            def _():
                push(2, s, q, across).wait_send()

        @pl.loop(0, chips)
        def _(which):
            push(3, which * 2 + core, q, partner).wait_send()


def mixer(features, taps, rates, residues, own_weight):
    n, m = lax.axis_size("ctx"), lax.axis_size("mp")
    length, channels = features.shape[1:]
    modes = rates.shape[0]
    depth, wide = own_weight.shape
    blocks = channels // LANES
    seg = length // ROWS
    chips = n // 2
    line = chips // SIDE
    parts = chips // m
    quarters = 4 if wide % (4 * LANES) == 0 and n <= 16 else 1
    dma = pltpu.SemaphoreType.DMA
    whole = pl.BlockSpec(memory_space=pltpu.VMEM)
    anywhere = pl.BlockSpec(memory_space=pl.ANY)
    return pl.pallas_call(
        lambda *refs: mixer_kernel(n, m, quarters, *refs),
        out_shape=jax.ShapeDtypeStruct((length, wide), jnp.bfloat16),
        in_specs=[anywhere, whole, whole, whole, anywhere],
        out_specs=whole,
        scratch_shapes=[
            pltpu.VMEM((3, length, channels), jnp.bfloat16),
            pltpu.VMEM((3, HALO, channels), jnp.bfloat16),
            pltpu.VMEM((3, ROWS * (seg + ROWS + 1) + ROWS, LANES), F32),
            pltpu.VMEM((blocks * seg, ROWS, LANES), F32),
            pltpu.VMEM((blocks * seg, ROWS, LANES), F32),
            pltpu.VMEM((blocks * modes, ROWS, LANES), F32),
            pltpu.VMEM((2, modes, channels), F32),
            pltpu.VMEM((modes, channels), F32),
            pltpu.VMEM((JUMP, modes, channels), F32),
            pltpu.VMEM((modes, channels // 2), F32),
            pltpu.VMEM((line, modes, channels // 2), F32),
            pltpu.VMEM((2, modes, channels // 2), F32),
            pltpu.VMEM((modes, channels), F32),
            pltpu.VMEM((n * depth, wide), jnp.bfloat16),
            pltpu.VMEM((m, length, channels), jnp.bfloat16),
            pltpu.VMEM((length, wide), F32),
            dma((4, n, quarters)),
            dma((n, quarters)),
            dma((4,)),
            dma((4,)),
            dma((line,)),
            dma((line,)),
            dma((m, parts)),
            dma((m, parts)),
            dma,
            dma,
            dma((parts,)),
            dma,
        ],
        compiler_params=pltpu.CompilerParams(
            collective_id=0, has_side_effects=True, vmem_limit_bytes=58 << 20
        ),
        name="mixer",
    )(features, taps, rates, residues, own_weight)


def body(features, short_filter, residues, rates, out_weight):
    return mixer(features, short_filter, rates.T, residues.T, out_weight)


def solution(mesh):
    placed = (
        P(None, "ctx", "mp"),
        P(None, None, "mp"),
        P("mp", None),
        P("mp", None),
        P("ctx", "mp"),
    )
    return jax.shard_map(
        body, mesh=mesh, in_specs=placed, out_specs=P("ctx", "mp"), check_vma=False
    )
```

```python
import jax
import jax.numpy as jnp
from jax import lax
from jax.experimental import pallas as pl
from jax.experimental.pallas import tpu as pltpu
from jax.sharding import PartitionSpec as P

LANES = 128
ROWS = 8
STEP = 8
HALO = 16
SIDE = 2
JUMP = 2 * SIDE
F32 = jnp.float32
MESH = pl.DeviceIdType.MESH


def one_minus_exp(x):
    series = jnp.ones_like(x)
    for k in range(11, 1, -1):
        series = 1.0 - x * (1.0 / k) * series
    return jnp.where(x < 0.5, x * series, 1.0 - jnp.exp(-x))


def mixer_kernel(n, m, quarters, feat, taps, rates, residues, own_weight, out,
                 stream, halo, ext, gated, fq, inclusive, decay, scaled, level, tot, behind, carried,
                 initial, weight, combined, total,
                 w_send, w_recv, s_send, s_recv, z_send, z_recv, x_send, x_recv, h_send, h_recv,
                 f_sem, k_sem):
    length, channels = feat.shape[1:]
    width = taps.shape[1]
    modes = rates.shape[0]
    depth, wide = own_weight.shape
    seg = length // ROWS
    pitch = seg + ROWS + 1
    blocks = channels // LANES
    chips = n // 2
    line = chips // SIDE
    per_group = chips // m
    parts = per_group
    part = channels // parts
    piece = wide // quarters
    half = channels // 2
    me, mine = lax.axis_index("ctx"), lax.axis_index("mp")
    core = lax.rem(me, 2)
    chip = lax.div(me, 2)
    b = lax.rem(chip, SIDE)
    a = lax.div(chip, SIDE)
    r = b * 2 + core
    partner = me + 1 - 2 * core
    across = me + 2 * (1 - 2 * b)
    up, down = a < line - 1, a > 0

    barrier = pltpu.get_barrier_semaphore()

    def greet(other, ok):
        @pl.when(ok)
        def _():
            pl.semaphore_signal(barrier, inc=1, device_id={"ctx": other}, device_id_type=MESH)

    greet(me + 1, me + 1 < n)
    greet(me - 1, me > 0)
    pl.semaphore_signal(barrier, inc=1, device_id={"ctx": across}, device_id_type=MESH)
    for k in range(1, line):
        greet(me + k * JUMP, a + k < line)
        greet(me - k * JUMP, a >= k)
    for k in range(1, m):
        pl.semaphore_signal(
            barrier, inc=1, device_id={"mp": lax.rem(mine + k, m)}, device_id_type=MESH
        )
    pl.semaphore_wait(
        barrier,
        1 + (line - 1) + (m - 1) + (me > 0).astype(jnp.int32) + (me < n - 1).astype(jnp.int32),
    )

    def columns(q):
        return pl.ds(pl.multiple_of(q * piece, piece), piece)

    def slot(s, q):
        return weight.at[pl.ds(pl.multiple_of(s * depth, depth), depth), columns(q)]

    def push(kind, s, q, to, own=False):
        return pltpu.make_async_remote_copy(
            src_ref=own_weight.at[:, columns(q)] if own else slot(s, q),
            dst_ref=slot(s, q),
            send_sem=w_send.at[kind, s, q],
            recv_sem=w_recv.at[s, q],
            device_id={"ctx": to},
            device_id_type=MESH,
        )

    def halo_copy():
        return pltpu.make_async_remote_copy(
            src_ref=feat.at[:, length - HALO :, :],
            dst_ref=halo,
            send_sem=h_send,
            recv_sem=h_recv,
            device_id={"ctx": lax.rem(me + 1, n)},
            device_id_type=MESH,
        )

    def load(p):
        where = pl.ds(pl.multiple_of(p * part, part), part)
        return pltpu.make_async_copy(feat.at[:, :, where], stream.at[:, :, where], f_sem.at[p])

    @pl.when(me < n - 1)
    def _():
        halo_copy().start()

    load(0).start()
    for q in range(quarters):
        @pl.when(up)
        def _():
            push(0, me, q, me + JUMP, own=True).start()

        @pl.when(down)
        def _():
            push(1, me, q, me - JUMP, own=True).start()

        push(2, me, q, across, own=True).start()
    for p in range(1, parts):
        load(p).start()
    for q in range(quarters):
        push(3, me, q, partner, own=True).start()
    keep = pltpu.make_async_copy(
        own_weight, weight.at[pl.ds(pl.multiple_of(me * depth, depth), depth), :], k_sem
    )
    keep.start()

    decay[0] = jnp.exp(-rates[...])
    decay[1] = jnp.exp(-rates[...] * seg)
    scaled[...] = residues[...] * jnp.sqrt(one_minus_exp(2.0 * rates[...]))

    @pl.when(me > 0)
    def _():
        halo_copy().wait_recv()

    @pl.when(me == 0)
    def _():
        halo[...] = jnp.zeros_like(halo)

    shape = (ROWS, LANES)
    row = lax.broadcasted_iota(jnp.int32, shape, 0)

    def lanes(c):
        return pl.ds(pl.multiple_of(c * LANES, LANES), LANES)

    def featurize(c):
        cols = lanes(c)
        for i in range(3):
            ext[i, :ROWS, :] = halo[i, :, cols].astype(F32)[HALO - ROWS :, :]
            for g in range(ROWS):
                ext[i, g * pitch + ROWS : g * pitch + ROWS + seg, :] = stream[
                    i, g * seg : (g + 1) * seg, cols
                ].astype(F32)
                if g:
                    ext[i, g * pitch : g * pitch + ROWS, :] = stream[
                        i, g * seg - HALO : g * seg, cols
                    ].astype(F32)[HALO - ROWS :, :]
        tap = [
            [jnp.broadcast_to(taps[i, j : j + 1, cols], shape) for j in range(width)]
            for i in range(3)
        ]

        @pl.loop(0, seg // STEP)
        def _(block):
            start = block * STEP
            made = []
            for i in range(3):
                rows = [
                    ext[i, pl.ds(start + k + ROWS - (width - 1), ROWS, stride=pitch), :]
                    for k in range(STEP + width - 1)
                ]
                made.append(
                    [
                        sum(
                            (tap[i][j] * rows[k + width - 1 - j] for j in range(1, width)),
                            tap[i][0] * rows[k + width - 1],
                        )
                        for k in range(STEP)
                    ]
                )
            for k in range(STEP):
                at = c * seg + start + k
                fq[at] = made[0][k]
                gated[at] = (made[1][k] * made[2][k]).astype(jnp.bfloat16).astype(F32)

        step_decay = [jnp.broadcast_to(decay[0, k : k + 1, cols], shape) for k in range(modes)]

        def advance(block, modal):
            for k in range(STEP):
                g = gated[c * seg + block * STEP + k]
                modal = tuple(d * s + g for d, s in zip(step_decay, modal))
            return modal

        modal = lax.fori_loop(0, seg // STEP, advance, (jnp.zeros(shape, F32),) * modes)
        for k in range(modes):
            value = modal[k]
            factor = jnp.broadcast_to(decay[1, k : k + 1, cols], shape)
            distance = 1
            while distance < ROWS:
                earlier = pltpu.roll(value, distance, 0)
                value = value + jnp.where(row >= distance, factor * earlier, 0.0)
                factor = factor * factor
                distance *= 2
            inclusive[c * modes + k] = value
            level[r, k : k + 1, cols] = value[ROWS - 1 :, :]

    @pl.loop(0, parts)
    def _(p):
        load(p).wait()

        @pl.loop(0, blocks // parts)
        def _(j):
            featurize(p * (blocks // parts) + j)

    def take(s, q):
        push(3, s, q, partner).wait_recv()

    def via_line(at, q):
        return (at > 0) & (at < line - 1) | (q >= quarters - quarters // 2)

    def serve_line(k, q):
        for sign, kind, onward in ((1, 0, up), (-1, 1, down)):
            @pl.when((a - sign * k >= 0) & (a - sign * k < line))
            def _():
                s = me - sign * k * JUMP
                take(s, q)

                @pl.when(onward)
                def _():
                    push(kind, s, q, me + sign * JUMP).start()

                if k == 1:
                    @pl.when(jnp.logical_not(via_line(a, q)))
                    def _():
                        push(2, s, q, across).start()
                else:
                    push(2, s, q, across).start()
                push(3, s, q, partner).start()

    def cross_on(q):
        @pl.when(up & via_line(a + 1, q))
        def _():
            push(0, across, q, me + JUMP).start()

        @pl.when(down & via_line(a - 1, q))
        def _():
            push(1, across, q, me - JUMP).start()

    inside = up & down

    def serve_cross(q):
        take(across, q)
        push(3, across, q, partner).start()

        @pl.when(jnp.logical_not(inside))
        def _():
            cross_on(q)

    def state_copy(kind, src, to, dst=None):
        return pltpu.make_async_remote_copy(
            src_ref=src,
            dst_ref=src if dst is None else dst,
            send_sem=s_send.at[kind],
            recv_sem=s_recv.at[kind],
            device_id={"ctx": to},
            device_id_type=MESH,
        )

    opposite = (1 - b) * 2 + core
    to_partner = state_copy(0, level.at[r], partner)
    to_across = state_copy(1, level.at[r], across)
    to_partner_too = state_copy(2, level.at[opposite], partner)
    to_partner_last = state_copy(3, carried.at[core], partner)
    to_across.start()
    to_partner.start()

    if line > 1:
        serve_line(1, 0)
    to_across.wait_recv()
    to_partner_too.start()
    to_partner.wait_recv()
    to_partner_too.wait_recv()

    halves = pl.ds(pl.multiple_of(core * half, half), half)
    fade_device = jnp.exp(rates[:, halves] * (-1.0 * length))
    value = level[0, :, halves]
    for k in range(1, JUMP):
        value = fade_device * value + level[k, :, halves]
    tot[...] = value
    carried[core] = jnp.zeros_like(tot)

    def ahead(k):
        return pltpu.make_async_remote_copy(
            src_ref=tot,
            dst_ref=behind.at[k],
            send_sem=z_send.at[k],
            recv_sem=z_recv.at[k],
            device_id={"ctx": lax.rem(me + k * JUMP, n)},
            device_id_type=MESH,
        )

    for k in range(1, line):
        @pl.when(a + k < line)
        def _():
            ahead(k).start()

    if line > 1:
        @pl.loop(1, quarters)
        def _(q):
            serve_line(1, q)

    @pl.loop(0, quarters)
    def _(q):
        serve_cross(q)

    for k in range(1, line):
        @pl.when(a >= k)
        def _():
            ahead(k).wait_recv()
            carried[core] += behind[k] * jnp.exp(
                rates[:, halves] * (-1.0 * length * JUMP * (k - 1))
            )

    to_partner_last.start()
    to_partner_last.wait_recv()
    for h in range(2):
        where = slice(h * half, (h + 1) * half)
        fade_device = jnp.exp(rates[:, where] * (-1.0 * length))
        value = carried[h]
        for k in range(JUMP - 1):
            value = jnp.where(r > k, fade_device * value + level[k, :, where], value)
        initial[:, where] = value

    def part_of(group, i):
        first = group * (per_group // SIDE)
        step = i // SIDE
        place = jnp.where(a <= first, step, per_group // SIDE - 1 - step)
        return place * SIDE + lax.rem(b + lax.rem(i, SIDE), SIDE)

    def swap(k, p):
        where = combined.at[mine, :, pl.ds(pl.multiple_of(p * part, part), part)]
        return pltpu.make_async_remote_copy(
            src_ref=where,
            dst_ref=where,
            send_sem=x_send.at[k, p],
            recv_sem=x_recv.at[mine, p],
            device_id={"mp": lax.rem(mine + k, m)},
            device_id_type=MESH,
        )

    offset = (row * seg).astype(F32)

    def finish(c):
        cols = lanes(c)
        starts = []
        for k in range(modes):
            before = jnp.where(row == 0, 0.0, pltpu.roll(inclusive[c * modes + k], 1, 0))
            fade = jnp.exp(-rates[k : k + 1, cols] * offset)
            starts.append(before + fade * initial[k : k + 1, cols])
        step_decay = [jnp.broadcast_to(decay[0, k : k + 1, cols], shape) for k in range(modes)]
        gain = [jnp.broadcast_to(scaled[k : k + 1, cols], shape) for k in range(modes)]

        def advance(block, modal):
            for k in range(STEP):
                t = block * STEP + k
                g = gated[c * seg + t]
                modal = tuple(d * s + g for d, s in zip(step_decay, modal))
                terms = [w * s for w, s in zip(gain, modal)]
                while len(terms) > 1:
                    terms = [sum(terms[i + 1 : i + 2], terms[i]) for i in range(0, len(terms), 2)]
                ext[0, pl.ds(t, ROWS, stride=pitch), :] = fq[c * seg + t] * terms[0]
            return modal

        lax.fori_loop(0, seg // STEP, advance, tuple(starts))
        for g in range(ROWS):
            combined[mine, g * seg : (g + 1) * seg, cols] = ext[
                0, g * pitch : g * pitch + seg, :
            ].astype(jnp.bfloat16)

    beside = quarters == parts and line > 2

    @pl.loop(0, parts)
    def _(i):
        p = part_of(mine, i)

        @pl.loop(0, blocks // parts)
        def _(j):
            finish(p * (blocks // parts) + j)

        for k in range(1, m):
            swap(k, p).start()
        if beside:
            serve_line(2, i)

    if line > 2 and not beside:
        @pl.loop(0, quarters)
        def _(q):
            serve_line(2, q)

    @pl.when(inside)
    def _():
        @pl.loop(0, quarters)
        def _(q):
            cross_on(q)

    keep.wait()

    def multiply(group, i, first=False, last=False):
        p = part_of(group, i)
        which = group * per_group + p
        there = lax.div(which, SIDE)

        @pl.when((lax.rem(which, SIDE) != b) & (there != a))
        def _():
            @pl.loop(0, quarters)
            def _(q):
                take(which * 2 + core, q)
                push(3, which * 2 + core, q, partner).start()

        rows = pl.ds(pl.multiple_of(which * 2 * depth, 2 * depth), 2 * depth)
        inner = pl.ds(pl.multiple_of(p * part, part), part)

        @pl.loop(0, quarters)
        def _(q):
            take(which * 2 + 1 - core, q)
            cols = columns(q)
            product = jnp.dot(
                combined[group, :, inner], weight[rows, cols], preferred_element_type=F32
            )
            if not first:
                product = total[:, cols] + product
            if last:
                out[:, cols] = product.astype(out.dtype)
            else:
                total[:, cols] = product

    def near(i, first=False):
        multiply(mine, i, first=first)

    def other(i, last=False):
        for k in range(1, m):
            group = lax.rem(mine + k, m)
            p = part_of(group, i)
            where = combined.at[group, :, pl.ds(pl.multiple_of(p * part, part), part)]
            pltpu.make_async_remote_copy(
                src_ref=where,
                dst_ref=where,
                send_sem=x_send.at[k, p],
                recv_sem=x_recv.at[group, p],
                device_id={"mp": group},
                device_id_type=MESH,
            ).wait_recv()
            multiply(group, i, last=last and k == m - 1)

    def serve_rest(q):
        for k in range(3, line):
            serve_line(k, q)

    if parts == 4 and quarters == 4:
        near(0, first=True)
        other(0)
        serve_rest(0)
        near(1)
        serve_rest(1)
        other(1)
        serve_rest(2)
        serve_rest(3)
        near(2)
        other(2)
        near(3)
        other(3, last=True)
    else:
        @pl.loop(0, quarters)
        def _(q):
            serve_rest(q)

        for i in range(parts):
            near(i, first=i == 0)
            other(i, last=i == parts - 1)

    @pl.when(me < n - 1)
    def _():
        halo_copy().wait_send()

    for copy in (to_partner, to_across, to_partner_too, to_partner_last):
        copy.wait_send()
    for k in range(1, line):
        @pl.when(a + k < line)
        def _():
            ahead(k).wait_send()

    for k in range(1, m):
        for p in range(parts):
            swap(k, p).wait_send()

    @pl.loop(0, quarters)
    def _(q):
        @pl.when(up & via_line(a + 1, q))
        def _():
            push(0, across, q, me + JUMP).wait_send()

        @pl.when(down & via_line(a - 1, q))
        def _():
            push(1, across, q, me - JUMP).wait_send()

        @pl.loop(0, line)
        def _(aa):
            s = (aa * SIDE + b) * 2 + core
            gap = jnp.abs(aa - a)

            @pl.when(up & (aa <= a))
            def _():
                push(0, s, q, me + JUMP).wait_send()

            @pl.when(down & (aa >= a))
            def _():
                push(1, s, q, me - JUMP).wait_send()

            @pl.when((gap != 1) | jnp.logical_not(via_line(a, q)))
            def _():
                push(2, s, q, across).wait_send()

        @pl.loop(0, chips)
        def _(which):
            push(3, which * 2 + core, q, partner).wait_send()


def mixer(features, taps, rates, residues, own_weight):
    n, m = lax.axis_size("ctx"), lax.axis_size("mp")
    length, channels = features.shape[1:]
    modes = rates.shape[0]
    depth, wide = own_weight.shape
    blocks = channels // LANES
    seg = length // ROWS
    chips = n // 2
    line = chips // SIDE
    parts = chips // m
    quarters = 4 if wide % (4 * LANES) == 0 and n <= 16 else 1
    dma = pltpu.SemaphoreType.DMA
    whole = pl.BlockSpec(memory_space=pltpu.VMEM)
    anywhere = pl.BlockSpec(memory_space=pl.ANY)
    return pl.pallas_call(
        lambda *refs: mixer_kernel(n, m, quarters, *refs),
        out_shape=pltpu.VMEM((length, wide), jnp.bfloat16),
        in_specs=[anywhere, whole, whole, whole, anywhere],
        out_specs=whole,
        scratch_shapes=[
            pltpu.VMEM((3, length, channels), jnp.bfloat16),
            pltpu.VMEM((3, HALO, channels), jnp.bfloat16),
            pltpu.VMEM((3, ROWS * (seg + ROWS + 1) + ROWS, LANES), F32),
            pltpu.VMEM((blocks * seg, ROWS, LANES), F32),
            pltpu.VMEM((blocks * seg, ROWS, LANES), F32),
            pltpu.VMEM((blocks * modes, ROWS, LANES), F32),
            pltpu.VMEM((2, modes, channels), F32),
            pltpu.VMEM((modes, channels), F32),
            pltpu.VMEM((JUMP, modes, channels), F32),
            pltpu.VMEM((modes, channels // 2), F32),
            pltpu.VMEM((line, modes, channels // 2), F32),
            pltpu.VMEM((2, modes, channels // 2), F32),
            pltpu.VMEM((modes, channels), F32),
            pltpu.VMEM((n * depth, wide), jnp.bfloat16),
            pltpu.VMEM((m, length, channels), jnp.bfloat16),
            pltpu.VMEM((length, wide), F32),
            dma((4, n, quarters)),
            dma((n, quarters)),
            dma((4,)),
            dma((4,)),
            dma((line,)),
            dma((line,)),
            dma((m, parts)),
            dma((m, parts)),
            dma,
            dma,
            dma((parts,)),
            dma,
        ],
        compiler_params=pltpu.CompilerParams(
            collective_id=0, has_side_effects=True, vmem_limit_bytes=52 << 20
        ),
        name="mixer",
    )(features, taps, rates, residues, own_weight)


def body(features, short_filter, residues, rates, out_weight):
    return mixer(features, short_filter, rates.T, residues.T, out_weight)


def solution(mesh):
    placed = (
        P(None, "ctx", "mp"),
        P(None, None, "mp"),
        P("mp", None),
        P("mp", None),
        P("ctx", "mp"),
    )
    return jax.shard_map(
        body, mesh=mesh, in_specs=placed, out_specs=P("ctx", "mp"), check_vma=False
    )
```

```python
import jax
import jax.numpy as jnp
from jax import lax
from jax.experimental import pallas as pl
from jax.experimental.pallas import tpu as pltpu
from jax.sharding import PartitionSpec as P

LANES = 128
ROWS = 8
STEP = 8
HALO = 16
SIDE = 2
JUMP = 2 * SIDE
F32 = jnp.float32
MESH = pl.DeviceIdType.MESH


def one_minus_exp(x):
    series = jnp.ones_like(x)
    for k in range(11, 1, -1):
        series = 1.0 - x * (1.0 / k) * series
    return jnp.where(x < 0.5, x * series, 1.0 - jnp.exp(-x))


def mixer_kernel(n, m, quarters, feat, taps, rates, residues, own_weight, out,
                 stream, halo, ext, gated, fq, inclusive, decay, scaled, level, both, tot, behind, carried,
                 initial, weight, combined, total,
                 w_send, w_recv, s_send, s_recv, z_send, z_recv, x_send, x_recv, h_send, h_recv,
                 f_sem, k_sem, hello):
    length, channels = feat.shape[1:]
    width = taps.shape[1]
    modes = rates.shape[0]
    depth, wide = own_weight.shape
    seg = length // ROWS
    pitch = seg + ROWS + 1
    blocks = channels // LANES
    chips = n // 2
    line = chips // SIDE
    per_group = chips // m
    parts = per_group
    part = channels // parts
    piece = wide // quarters
    half = channels // 2
    me, mine = lax.axis_index("ctx"), lax.axis_index("mp")
    core = lax.rem(me, 2)
    chip = lax.div(me, 2)
    b = lax.rem(chip, SIDE)
    a = lax.div(chip, SIDE)
    partner = me + 1 - 2 * core
    across = me + 2 * (1 - 2 * b)
    up, down = a < line - 1, a > 0

    barrier = pltpu.get_barrier_semaphore()

    def greet(other, ok):
        @pl.when(ok)
        def _():
            pl.semaphore_signal(barrier, inc=1, device_id={"ctx": other}, device_id_type=MESH)

    greet(me + 1, me + 1 < n)
    greet(me - 1, me > 0)
    pl.semaphore_signal(barrier, inc=1, device_id={"ctx": across}, device_id_type=MESH)
    greet(me + JUMP, up)
    greet(me - JUMP, down)
    for k in range(1, m):
        pl.semaphore_signal(
            barrier, inc=1, device_id={"mp": lax.rem(mine + k, m)}, device_id_type=MESH
        )
    pl.semaphore_wait(
        barrier,
        m
        + sum(there.astype(jnp.int32) for there in (me > 0, me < n - 1, up, down)),
    )

    def signal_down(level_of, ok):
        @pl.when(ok & down)
        def _():
            pl.semaphore_signal(
                hello.at[level_of], inc=1, device_id={"ctx": me - JUMP}, device_id_type=MESH
            )

    if line > 2:
        signal_down(1, up)

    def columns(q):
        return pl.ds(pl.multiple_of(q * piece, piece), piece)

    def slot(s, q):
        return weight.at[pl.ds(pl.multiple_of(s * depth, depth), depth), columns(q)]

    def push(kind, s, q, to, own=False):
        return pltpu.make_async_remote_copy(
            src_ref=own_weight.at[:, columns(q)] if own else slot(s, q),
            dst_ref=slot(s, q),
            send_sem=w_send.at[kind, s, q],
            recv_sem=w_recv.at[s, q],
            device_id={"ctx": to},
            device_id_type=MESH,
        )

    def halo_copy():
        return pltpu.make_async_remote_copy(
            src_ref=feat.at[:, length - HALO :, :],
            dst_ref=halo,
            send_sem=h_send,
            recv_sem=h_recv,
            device_id={"ctx": lax.rem(me + 1, n)},
            device_id_type=MESH,
        )

    def load(p):
        where = pl.ds(pl.multiple_of(p * part, part), part)
        return pltpu.make_async_copy(feat.at[:, :, where], stream.at[:, :, where], f_sem.at[p])

    @pl.when(me < n - 1)
    def _():
        halo_copy().start()

    held = quarters - 1 if quarters > 1 else quarters

    def push_up(q):
        @pl.when(up)
        def _():
            push(0, me, q, me + JUMP, own=True).start()

    load(0).start()
    for q in range(quarters):
        if q < held:
            push_up(q)

        @pl.when(down)
        def _():
            push(1, me, q, me - JUMP, own=True).start()

        if q < held:
            push(2, me, q, across, own=True).start()
    for p in range(1, parts):
        load(p).start()
    for q in range(quarters):
        push(3, me, q, partner, own=True).start()
    keep = pltpu.make_async_copy(
        own_weight, weight.at[pl.ds(pl.multiple_of(me * depth, depth), depth), :], k_sem
    )
    keep.start()

    decay[0] = jnp.exp(-rates[...])
    decay[1] = jnp.exp(-rates[...] * seg)
    scaled[...] = residues[...] * jnp.sqrt(one_minus_exp(2.0 * rates[...]))

    @pl.when(me > 0)
    def _():
        halo_copy().wait_recv()

    @pl.when(me == 0)
    def _():
        halo[...] = jnp.zeros_like(halo)

    for k in range(2, line):
        @pl.when(a + k < line)
        def _():
            pl.semaphore_wait(hello.at[k - 1], 1)
            signal_down(k, a + k < line)

    shape = (ROWS, LANES)
    row = lax.broadcasted_iota(jnp.int32, shape, 0)

    def lanes(c):
        return pl.ds(pl.multiple_of(c * LANES, LANES), LANES)

    def featurize(c):
        cols = lanes(c)
        for i in range(3):
            ext[i, :ROWS, :] = halo[i, :, cols].astype(F32)[HALO - ROWS :, :]
            for g in range(ROWS):
                ext[i, g * pitch + ROWS : g * pitch + ROWS + seg, :] = stream[
                    i, g * seg : (g + 1) * seg, cols
                ].astype(F32)
                if g:
                    ext[i, g * pitch : g * pitch + ROWS, :] = stream[
                        i, g * seg - HALO : g * seg, cols
                    ].astype(F32)[HALO - ROWS :, :]
        tap = [
            [jnp.broadcast_to(taps[i, j : j + 1, cols], shape) for j in range(width)]
            for i in range(3)
        ]

        @pl.loop(0, seg // STEP)
        def _(block):
            start = block * STEP
            made = []
            for i in range(3):
                rows = [
                    ext[i, pl.ds(start + k + ROWS - (width - 1), ROWS, stride=pitch), :]
                    for k in range(STEP + width - 1)
                ]
                made.append(
                    [
                        sum(
                            (tap[i][j] * rows[k + width - 1 - j] for j in range(1, width)),
                            tap[i][0] * rows[k + width - 1],
                        )
                        for k in range(STEP)
                    ]
                )
            for k in range(STEP):
                at = c * seg + start + k
                fq[at] = made[0][k]
                gated[at] = (made[1][k] * made[2][k]).astype(jnp.bfloat16).astype(F32)

        step_decay = [jnp.broadcast_to(decay[0, k : k + 1, cols], shape) for k in range(modes)]

        def advance(block, modal):
            for k in range(STEP):
                g = gated[c * seg + block * STEP + k]
                modal = tuple(d * s + g for d, s in zip(step_decay, modal))
            return modal

        modal = lax.fori_loop(0, seg // STEP, advance, (jnp.zeros(shape, F32),) * modes)
        for k in range(modes):
            value = modal[k]
            factor = jnp.broadcast_to(decay[1, k : k + 1, cols], shape)
            distance = 1
            while distance < ROWS:
                earlier = pltpu.roll(value, distance, 0)
                value = value + jnp.where(row >= distance, factor * earlier, 0.0)
                factor = factor * factor
                distance *= 2
            inclusive[c * modes + k] = value
            level[core, k : k + 1, cols] = value[ROWS - 1 :, :]

    @pl.loop(0, parts)
    def _(p):
        load(p).wait()

        @pl.loop(0, blocks // parts)
        def _(j):
            featurize(p * (blocks // parts) + j)

    def take(s, q):
        push(3, s, q, partner).wait_recv()

    def via_line(at, q):
        return (at > 0) & (at < line - 1) | (q >= quarters - quarters // 2)

    def serve_line(k, q, signs=(1, -1)):
        for sign in signs:
            onward = up if sign == 1 else down

            @pl.when((a - sign * k >= 0) & (a - sign * k < line))
            def _():
                s = me - sign * k * JUMP
                take(s, q)

                @pl.when(onward)
                def _():
                    push((1 - sign) // 2, s, q, me + sign * JUMP).start()

                if k == 1:
                    @pl.when(jnp.logical_not(via_line(a, q)))
                    def _():
                        push(2, s, q, across).start()
                else:
                    push(2, s, q, across).start()
                push(3, s, q, partner).start()

    def cross_on(q):
        @pl.when(up & via_line(a + 1, q))
        def _():
            push(0, across, q, me + JUMP).start()

        @pl.when(down & via_line(a - 1, q))
        def _():
            push(1, across, q, me - JUMP).start()

    inside = up & down

    def serve_cross(q):
        take(across, q)
        push(3, across, q, partner).start()

        @pl.when(jnp.logical_not(inside))
        def _():
            cross_on(q)

    def state_copy(kind, src, to, dst=None):
        return pltpu.make_async_remote_copy(
            src_ref=src,
            dst_ref=src if dst is None else dst,
            send_sem=s_send.at[kind],
            recv_sem=s_recv.at[kind],
            device_id={"ctx": to},
            device_id_type=MESH,
        )

    halves = pl.ds(pl.multiple_of(core * half, half), half)

    def fade(devices, where):
        return jnp.exp(rates[:, where] * (-1.0 * length * devices))

    def ahead(k):
        return pltpu.make_async_remote_copy(
            src_ref=tot,
            dst_ref=behind.at[k],
            send_sem=z_send.at[k],
            recv_sem=z_recv.at[k],
            device_id={"ctx": lax.rem(me + k * JUMP, n)},
            device_id_type=MESH,
        )

    to_partner = state_copy(0, level.at[core], partner)
    to_across = state_copy(1, both.at[b], across)
    to_partner_last = state_copy(2, carried.at[core], partner)
    to_partner.start()
    for q in range(held, quarters):
        push_up(q)
    to_partner.wait_recv()
    both[b] = fade(1, halves) * level[0, :, halves] + level[1, :, halves]
    to_across.start()
    for q in range(held, quarters):
        push(2, me, q, across, own=True).start()
    soon = quarters - 1
    if line > 1:
        @pl.loop(0, soon)
        def _(q):
            serve_line(1, q, (-1,))

    to_across.wait_recv()
    tot[...] = fade(2, halves) * both[0] + both[1]
    for k in range(1, line):
        @pl.when(a + k < line)
        def _():
            ahead(k).start()

    if line > 1:
        @pl.loop(0, quarters - 1)
        def _(q):
            serve_line(1, q, (1,))

        @pl.loop(soon, quarters - 1)
        def _(q):
            serve_line(1, q, (-1,))

    @pl.loop(0, quarters - 1)
    def _(q):
        serve_cross(q)

    carried[core] = jnp.zeros_like(tot)
    for k in range(1, line):
        @pl.when(a >= k)
        def _():
            ahead(k).wait_recv()
            carried[core] += behind[k] * fade(JUMP * (k - 1), halves)

    @pl.when(b == 1)
    def _():
        carried[core] = fade(2, halves) * carried[core] + both[0]

    to_partner_last.start()
    to_partner_last.wait_recv()
    for h in range(2):
        where = slice(h * half, (h + 1) * half)
        value = carried[h]
        initial[:, where] = jnp.where(
            core == 1, fade(1, where) * value + level[0, :, where], value
        )

    def part_of(group, i):
        first = group * (per_group // SIDE)
        step = i // SIDE
        place = jnp.where(a <= first, step, per_group // SIDE - 1 - step)
        return place * SIDE + lax.rem(b + lax.rem(i, SIDE), SIDE)

    def swap(k, p):
        where = combined.at[mine, :, pl.ds(pl.multiple_of(p * part, part), part)]
        return pltpu.make_async_remote_copy(
            src_ref=where,
            dst_ref=where,
            send_sem=x_send.at[k, p],
            recv_sem=x_recv.at[mine, p],
            device_id={"mp": lax.rem(mine + k, m)},
            device_id_type=MESH,
        )

    offset = (row * seg).astype(F32)

    def finish(c):
        cols = lanes(c)
        starts = []
        for k in range(modes):
            before = jnp.where(row == 0, 0.0, pltpu.roll(inclusive[c * modes + k], 1, 0))
            faded = jnp.exp(-rates[k : k + 1, cols] * offset)
            starts.append(before + faded * initial[k : k + 1, cols])
        step_decay = [jnp.broadcast_to(decay[0, k : k + 1, cols], shape) for k in range(modes)]
        gain = [jnp.broadcast_to(scaled[k : k + 1, cols], shape) for k in range(modes)]

        def advance(block, modal):
            for k in range(STEP):
                t = block * STEP + k
                g = gated[c * seg + t]
                modal = tuple(d * s + g for d, s in zip(step_decay, modal))
                terms = [w * s for w, s in zip(gain, modal)]
                while len(terms) > 1:
                    terms = [sum(terms[i + 1 : i + 2], terms[i]) for i in range(0, len(terms), 2)]
                ext[0, pl.ds(t, ROWS, stride=pitch), :] = fq[c * seg + t] * terms[0]
            return modal

        lax.fori_loop(0, seg // STEP, advance, tuple(starts))
        for g in range(ROWS):
            combined[mine, g * seg : (g + 1) * seg, cols] = ext[
                0, g * pitch : g * pitch + seg, :
            ].astype(jnp.bfloat16)

    @pl.loop(0, parts)
    def _(i):
        p = part_of(mine, i)

        @pl.loop(0, blocks // parts)
        def _(j):
            finish(p * (blocks // parts) + j)

        for k in range(1, m):
            swap(k, p).start()

        @pl.when(i == 0)
        def _():
            if line > 1:
                serve_line(1, quarters - 1)
            serve_cross(quarters - 1)

        if quarters == parts and line > 2:
            serve_line(2, i)

    if line > 2 and quarters != parts:
        @pl.loop(0, quarters)
        def _(q):
            serve_line(2, q)

    @pl.when(inside)
    def _():
        @pl.loop(0, quarters)
        def _(q):
            cross_on(q)

    keep.wait()

    def place(group, i):
        p = part_of(group, i)
        return p, group * per_group + p

    def fetch(group, i, q):
        _, which = place(group, i)

        @pl.when((lax.rem(which, SIDE) != b) & (lax.div(which, SIDE) != a))
        def _():
            take(which * 2 + core, q)
            push(3, which * 2 + core, q, partner).start()

    def multiply(group, i, q, first=False, last=False):
        p, which = place(group, i)
        take(which * 2 + 1 - core, q)
        rows = pl.ds(pl.multiple_of(which * 2 * depth, 2 * depth), 2 * depth)
        inner = pl.ds(pl.multiple_of(p * part, part), part)
        cols = columns(q)
        product = jnp.dot(
            combined[group, :, inner], weight[rows, cols], preferred_element_type=F32
        )
        if not first:
            product = total[:, cols] + product
        if last:
            out[:, cols] = product.astype(out.dtype)
        else:
            total[:, cols] = product

    others = [lax.rem(mine + k, m) for k in range(1, m)]

    def arrive(k, i):
        group = others[k - 1]
        p = part_of(group, i)
        where = combined.at[group, :, pl.ds(pl.multiple_of(p * part, part), part)]
        pltpu.make_async_remote_copy(
            src_ref=where,
            dst_ref=where,
            send_sem=x_send.at[k, p],
            recv_sem=x_recv.at[group, p],
            device_id={"mp": group},
            device_id_type=MESH,
        ).wait_recv()

    def chip_of(group, i, first=False):
        @pl.loop(0, quarters)
        def _(q):
            fetch(group, i, q)

        @pl.loop(0, quarters)
        def _(q):
            multiply(group, i, q, first=first)

    def near(i, first=False):
        chip_of(mine, i, first=first)

    def other(i):
        for k in range(1, m):
            arrive(k, i)
            chip_of(others[k - 1], i)

    def serve_rest(q):
        for k in range(3, line):
            serve_line(k, q)

    if parts == 4 and quarters == 4:
        near(0, first=True)
        other(0)
        serve_rest(0)
        serve_rest(1)
        near(1)
        other(1)
        serve_rest(2)
        serve_rest(3)
        near(2)
        other(2)
    else:
        @pl.loop(0, quarters)
        def _(q):
            serve_rest(q)

        for i in range(parts - 1):
            near(i, first=i == 0)
            other(i)

    for k in range(1, m):
        arrive(k, parts - 1)
    groups = (mine, *others)
    for group in groups:
        fetch(group, parts - 1, 0)
    for q in range(quarters):
        for group in groups:
            if q + 1 < quarters:
                fetch(group, parts - 1, q + 1)
        for k, group in enumerate(groups):
            multiply(group, parts - 1, q, first=parts == 1 and k == 0, last=k == m - 1)

    @pl.when(me < n - 1)
    def _():
        halo_copy().wait_send()

    for copy in (to_partner, to_across, to_partner_last):
        copy.wait_send()
    for k in range(1, line):
        @pl.when(a + k < line)
        def _():
            ahead(k).wait_send()

    for k in range(1, m):
        for p in range(parts):
            swap(k, p).wait_send()

    @pl.loop(0, quarters)
    def _(q):
        @pl.when(up & via_line(a + 1, q))
        def _():
            push(0, across, q, me + JUMP).wait_send()

        @pl.when(down & via_line(a - 1, q))
        def _():
            push(1, across, q, me - JUMP).wait_send()

        @pl.loop(0, line)
        def _(aa):
            s = (aa * SIDE + b) * 2 + core
            gap = jnp.abs(aa - a)

            @pl.when(up & (aa <= a))
            def _():
                push(0, s, q, me + JUMP).wait_send()

            @pl.when(down & (aa >= a))
            def _():
                push(1, s, q, me - JUMP).wait_send()

            @pl.when((gap != 1) | jnp.logical_not(via_line(a, q)))
            def _():
                push(2, s, q, across).wait_send()

        @pl.loop(0, chips)
        def _(which):
            push(3, which * 2 + core, q, partner).wait_send()


def mixer(features, taps, rates, residues, own_weight):
    n, m = lax.axis_size("ctx"), lax.axis_size("mp")
    length, channels = features.shape[1:]
    modes = rates.shape[0]
    depth, wide = own_weight.shape
    blocks = channels // LANES
    seg = length // ROWS
    chips = n // 2
    line = chips // SIDE
    parts = chips // m
    quarters = 4 if wide % (4 * LANES) == 0 and n <= 16 else 1
    dma = pltpu.SemaphoreType.DMA
    whole = pl.BlockSpec(memory_space=pltpu.VMEM)
    anywhere = pl.BlockSpec(memory_space=pl.ANY)
    return pl.pallas_call(
        lambda *refs: mixer_kernel(n, m, quarters, *refs),
        out_shape=pltpu.VMEM((length, wide), jnp.bfloat16),
        in_specs=[anywhere, whole, whole, whole, anywhere],
        out_specs=whole,
        scratch_shapes=[
            pltpu.VMEM((3, length, channels), jnp.bfloat16),
            pltpu.VMEM((3, HALO, channels), jnp.bfloat16),
            pltpu.VMEM((3, ROWS * (seg + ROWS + 1) + ROWS, LANES), F32),
            pltpu.VMEM((blocks * seg, ROWS, LANES), F32),
            pltpu.VMEM((blocks * seg, ROWS, LANES), F32),
            pltpu.VMEM((blocks * modes, ROWS, LANES), F32),
            pltpu.VMEM((2, modes, channels), F32),
            pltpu.VMEM((modes, channels), F32),
            pltpu.VMEM((2, modes, channels), F32),
            pltpu.VMEM((2, modes, channels // 2), F32),
            pltpu.VMEM((modes, channels // 2), F32),
            pltpu.VMEM((line, modes, channels // 2), F32),
            pltpu.VMEM((2, modes, channels // 2), F32),
            pltpu.VMEM((modes, channels), F32),
            pltpu.VMEM((n * depth, wide), jnp.bfloat16),
            pltpu.VMEM((m, length, channels), jnp.bfloat16),
            pltpu.VMEM((length, wide), F32),
            dma((4, n, quarters)),
            dma((n, quarters)),
            dma((3,)),
            dma((3,)),
            dma((line,)),
            dma((line,)),
            dma((m, parts)),
            dma((m, parts)),
            dma,
            dma,
            dma((parts,)),
            dma,
            pltpu.SemaphoreType.REGULAR((line,)),
        ],
        compiler_params=pltpu.CompilerParams(
            collective_id=0, has_side_effects=True, vmem_limit_bytes=52 << 20
        ),
        name="mixer",
    )(features, taps, rates, residues, own_weight)


def body(features, short_filter, residues, rates, out_weight):
    return mixer(features, short_filter, rates.T, residues.T, out_weight)


def solution(mesh):
    placed = (
        P(None, "ctx", "mp"),
        P(None, None, "mp"),
        P("mp", None),
        P("mp", None),
        P("ctx", "mp"),
    )
    return jax.shard_map(
        body, mesh=mesh, in_specs=placed, out_specs=P("ctx", "mp"), check_vma=False
    )
```
